32 devices in a mesh: region: 8 (over y, x, core), group: 4 (over z).
Axes of the slice: x: 2, y: 2, z: 4, core: 2. Of those that a mesh axis runs over, the one named last changes fastest.
Arguments:
- ensemble: bfloat16 [8192, 512], P(('region', 'group')), may hold values from -6 to 6
- tiles: bfloat16 [2, 256, 8192], P(None, None, ('region', 'group')), may hold values from -0.09375 to 0.09375
- tile_live: int32 [2, 8], replicated, may hold values 0 or 1
- observed: float32 [2, 256], replicated, may hold values from -6 to 6
- perturb: bfloat16 [2, 256, 512], replicated, may hold values from -6 to 6
- obs_var: float32 [2, 256], replicated, may hold values from 0.5 to 4
Outputs:
- analysis: bfloat16 [8192, 512], P(('region', 'group'))
The draws below stay inside these ranges and needn't reach their ends.
All inputs are finite; a program needn't handle non-finite values. Where the reference program divides by a largest or mean magnitude, that divisor is 1e-20 or more.
Results may differ from the reference program's by a relative error of at most 0.013.
Values may be sent and summed in bfloat16 or wider, within the bound.
A program may use at most 64 MiB of HBM per device.

```python
import math
import jax
import jax.numpy as jnp
from jax import lax

VAR_DEV = 256
M = 512
P_SIZE = 256
BATCHES = 2
NEWTON = 4
REGIONS = 8
GROUPS = 4
VARS = 8192


def touch_ends(entries, rng, low, high):
    index_at = [jax.random.randint(jax.random.fold_in(rng, axis), (), 0, length) for axis, length in enumerate(entries.shape)]
    main_axis = entries.shape.index(max(entries.shape))
    neighbour = index_at[:main_axis] + [(index_at[main_axis] + 1) % entries.shape[main_axis]] + index_at[main_axis + 1:]
    return entries.at[tuple(index_at)].set(low).at[tuple(neighbour)].set(high)


def levels(rng, extent, cuts, least, high):
    level = 1.0
    for axis_at, blocks in cuts:
        draws = jax.random.uniform(jax.random.fold_in(jax.random.fold_in(rng, 6), axis_at), (blocks,), jnp.float32, least / len(cuts), high / len(cuts))
        level = level * jnp.repeat(jnp.exp(draws), extent[axis_at] // blocks).reshape((-1,) + (1,) * (len(extent) - 1 - axis_at))
    return level


def normal_values(key, dims, scale, most, split=(), kind=jnp.bfloat16):
    loudness = levels(key, dims, split, -0.22, 0.18) if split else 1.0
    drawn = jax.random.normal(key, dims, jnp.float32) * scale * loudness
    return jnp.minimum(jnp.maximum(drawn, -most), most).astype(kind)


def setup_inputs(seed: int = 0) -> dict:
    key_of = jax.random.split(jax.random.key(seed), 7)
    ensemble = normal_values(key_of[0], (VARS, M), 1.0, 6.0, ((0, 32),))
    tiles = normal_values(key_of[1], (BATCHES, P_SIZE, VARS), (VARS // 2) ** -0.5, 0.09375, ((2, 32),))
    tile_live = touch_ends((jax.random.randint(key_of[2], (BATCHES, REGIONS), 0, 2) < 1).astype(jnp.int32), jax.random.fold_in(key_of[2], 1), 0, 1)
    observed = normal_values(key_of[3], (BATCHES, P_SIZE), 1.0, 6.0, (), jnp.float32)
    perturb = normal_values(key_of[4], (BATCHES, P_SIZE, M), 1.0, 6.0)
    obs_var = jnp.clip(jnp.exp(jax.random.uniform(key_of[5], (BATCHES, P_SIZE), jnp.float32, math.log(0.5), math.log(4.0))), 0.5, 4.0)
    return dict(ensemble=ensemble, tiles=tiles, tile_live=tile_live, observed=observed, perturb=perturb, obs_var=obs_var)


def newton_weights(pred, obs_row, perturb_b, var_row):
    spread = pred - jnp.mean(pred, axis=1, keepdims=True)
    cov = jnp.dot(spread, spread.T, precision=lax.Precision.HIGHEST) / (M - 1) + jnp.diag(var_row)
    bound = jnp.max(jnp.sum(jnp.abs(cov), axis=1))
    ident = jnp.eye(P_SIZE, dtype=jnp.float32)
    approx = ident / bound
    for step in range(NEWTON):
        inner = 2.0 * ident - jnp.dot(cov, approx, precision=lax.Precision.HIGHEST)
        approx = jnp.dot(approx, inner, precision=lax.Precision.HIGHEST)
    innov = obs_row[:, None] + perturb_b.astype(jnp.float32) - pred
    weights = jnp.dot(approx, innov, precision=lax.Precision.HIGHEST).astype(jnp.bfloat16)
    return spread.astype(jnp.bfloat16), weights


def reference(ensemble, tiles, tile_live, observed, perturb, obs_var):
    state = ensemble
    for batch in range(BATCHES):
        rows = jnp.repeat(tile_live[batch], VAR_DEV * GROUPS).astype(jnp.bfloat16)
        live = state * rows[:, None]
        pred = jnp.dot(tiles[batch], live, preferred_element_type=jnp.float32)
        spread_low, weights = newton_weights(pred, observed[batch], perturb[batch], obs_var[batch])
        wide = state.astype(jnp.float32)
        anom = (wide - jnp.mean(wide, axis=1, keepdims=True)).astype(jnp.bfloat16)
        gain = (jnp.dot(anom, spread_low.T, preferred_element_type=jnp.float32) / (M - 1)).astype(jnp.bfloat16)
        state = (wide + jnp.dot(gain, weights, preferred_element_type=jnp.float32)).astype(jnp.bfloat16)
    return state
```

```python
import functools

import jax
import jax.numpy as jnp
from jax import lax
from jax.experimental import pallas as pl
from jax.experimental.pallas import tpu as pltpu
from jax.sharding import PartitionSpec as P

NEWTON = 4
F32 = jnp.float32
BF16 = jnp.bfloat16


def split(x):
    hi = x.astype(BF16)
    return hi, (x - hi.astype(F32)).astype(BF16)


def dot3(a, b):
    left = jnp.concatenate([a[0], a[0], a[1]], axis=1)
    right = jnp.concatenate([b[0], b[1], b[0]], axis=0)
    return jnp.dot(left, right, preferred_element_type=F32)


def dot_nt(a, b):
    return lax.dot_general(a, b, (((1,), (1,)), ((), ())), preferred_element_type=F32)


def kernel(
    region_count, group_count,
    ens_hbm, tiles_hbm, live_ref, obs_ref, pert_hbm, var_ref,
    out_ref,
    ens, tiles, pert, partial, rs_buf, z_send, z_buf, spread_buf,
    mean_part, mean_rs, mean_zsend, mean_z,
    load_sem, rs_ssem, rs_rsem, z_ssem, z_rsem, ag_ssem, ag_rsem,
    mrs_ssem, mrs_rsem, mz_ssem, mz_rsem,
):
    batches, obs_count, members = pert.shape
    region = lax.axis_index("region")
    group = lax.axis_index("group")
    chunk_rows, chunk_cols = rs_buf.shape[2:]
    across = members // chunk_cols

    barrier = pltpu.get_barrier_semaphore()
    for k in range(1, region_count):
        pl.semaphore_signal(barrier, inc=1, device_id=(lax.rem(region + k, region_count), group), device_id_type=pl.DeviceIdType.MESH)
    for k in range(1, group_count):
        pl.semaphore_signal(barrier, inc=1, device_id=(region, lax.rem(group + k, group_count)), device_id_type=pl.DeviceIdType.MESH)

    loads = [pltpu.make_async_copy(ens_hbm, ens, load_sem.at[0])]
    loads += [pltpu.make_async_copy(tiles_hbm.at[b], tiles.at[b], load_sem.at[1 + b]) for b in range(batches)]
    loads += [pltpu.make_async_copy(pert_hbm.at[b], pert.at[b], load_sem.at[1 + batches + b]) for b in range(batches)]
    for load in loads:
        load.start()

    row_at = lax.broadcasted_iota(jnp.int32, (obs_count, obs_count), 0)
    col_at = lax.broadcasted_iota(jnp.int32, (obs_count, obs_count), 1)
    on_diag = row_at == col_at
    ident = jnp.where(on_diag, 1.0, 0.0).astype(F32)

    def as_row(column):
        return jnp.sum(jnp.where(on_diag, column, 0.0), axis=0, keepdims=True)

    def as_column(row):
        return jnp.sum(jnp.where(on_diag, row, 0.0), axis=1, keepdims=True)

    def chunk(ref, index):
        rows = pl.ds(pl.multiple_of(lax.div(index, across) * chunk_rows, chunk_rows), chunk_rows)
        if across == 1:
            return ref.at[rows, :]
        return ref.at[rows, pl.ds(pl.multiple_of(lax.rem(index, across) * chunk_cols, chunk_cols), chunk_cols)]

    def remote(src, dst, ssem, rsem, where):
        return pltpu.make_async_remote_copy(
            src_ref=src, dst_ref=dst, send_sem=ssem, recv_sem=rsem,
            device_id=where, device_id_type=pl.DeviceIdType.MESH,
        )

    region_peers = [lax.rem(region + k, region_count) for k in range(1, region_count)]
    group_peers = [lax.rem(group + k, group_count) for k in range(1, group_count)]
    sends = []

    def launch(copy):
        copy.start()
        sends.append(copy)

    def local_partial(b):
        loads[1 + b].wait()
        value = jnp.dot(tiles[b], ens[...], preferred_element_type=F32)
        value = value * live_ref[b, region].astype(F32)
        mean = jnp.mean(value, axis=1, keepdims=True)
        partial[b] = (value - mean).astype(BF16)
        mean_part[:, b * obs_count:(b + 1) * obs_count] = as_row(mean)

    def scatter(b):
        for k, peer in enumerate(region_peers):
            launch(remote(chunk(partial.at[b], peer), rs_buf.at[b, region], rs_ssem.at[b, k], rs_rsem.at[b, region], (peer, group)))

    def sum_region(b):
        total = chunk(partial.at[b], region)[...].astype(F32)
        for peer in region_peers:
            remote(rs_buf.at[b, peer], rs_buf.at[b, peer], rs_ssem.at[b, 0], rs_rsem.at[b, peer], (peer, group)).wait_recv()
            total = total + rs_buf[b, peer].astype(F32)
        z_send[b] = total.astype(BF16)
        for k, peer in enumerate(group_peers):
            launch(remote(z_send.at[b], z_buf.at[b, group], z_ssem.at[b, k], z_rsem.at[b, group], (region, peer)))

    def sum_group(b):
        total = z_send[b].astype(F32)
        for peer in group_peers:
            remote(z_buf.at[b, peer], z_buf.at[b, peer], z_ssem.at[b, 0], z_rsem.at[b, peer], (region, peer)).wait_recv()
            total = total + z_buf[b, peer].astype(F32)
        mine = chunk(spread_buf.at[b], region)
        mine[...] = total.astype(BF16)
        for k, peer in enumerate(region_peers):
            launch(remote(mine, mine, ag_ssem.at[b, k], ag_rsem.at[b, region], (peer, group)))

    def gathered(b):
        for peer in region_peers:
            block = chunk(spread_buf.at[b], peer)
            remote(block, block, ag_ssem.at[b, 0], ag_rsem.at[b, peer], (peer, group)).wait_recv()
        return spread_buf[b]

    loads[0].wait()
    local_partial(0)
    pl.semaphore_wait(barrier, region_count - 1 + group_count - 1)
    scatter(0)
    for b in range(1, batches):
        local_partial(b)
    for k, peer in enumerate(region_peers):
        launch(remote(mean_part, mean_rs.at[region], mrs_ssem.at[k], mrs_rsem.at[region], (peer, group)))
    for b in range(1, batches):
        scatter(b)

    sum_region(0)
    total = mean_part[...]
    for peer in region_peers:
        remote(mean_rs.at[peer], mean_rs.at[peer], mrs_ssem.at[0], mrs_rsem.at[peer], (peer, group)).wait_recv()
        total = total + mean_rs[peer]
    mean_zsend[...] = total
    for k, peer in enumerate(group_peers):
        launch(remote(mean_zsend, mean_z.at[group], mz_ssem.at[k], mz_rsem.at[group], (region, peer)))
    for b in range(1, batches):
        sum_region(b)
    sum_group(0)
    mean_row = mean_zsend[...]
    for peer in group_peers:
        remote(mean_z.at[peer], mean_z.at[peer], mz_ssem.at[0], mz_rsem.at[peer], (region, peer)).wait_recv()
        mean_row = mean_row + mean_z[peer]
    for b in range(1, batches):
        sum_group(b)

    def anomaly(wide):
        return (wide - jnp.mean(wide, axis=1, keepdims=True)).astype(BF16)

    def newton_weights(spread_low, mismatch, shift, b):
        cov = dot_nt(spread_low, spread_low) / (members - 1) + jnp.where(on_diag, var_ref[b:b + 1, :], 0.0)
        bound = jnp.max(jnp.sum(jnp.abs(cov), axis=1, keepdims=True), axis=0, keepdims=True)
        residual = ident - cov / bound
        approx = ident + residual
        for step in range(1, NEWTON):
            parts = split(residual)
            residual = dot3(parts, parts)
            approx = approx + dot3(split(approx), split(residual))
        innov = mismatch + shift
        return (dot3(split(approx), split(innov)) / bound).astype(BF16)

    state = ens[...].astype(F32)
    anom = anomaly(state)
    offsets = [
        as_column(obs_ref[b:b + 1, :] - mean_row[:, b * obs_count:(b + 1) * obs_count]) for b in range(batches)
    ]
    history = []
    for b in range(batches):
        loads[1 + batches + b].wait()
        prior = gathered(b)
        spread = prior.astype(F32)
        for earlier_low, earlier_weights in history:
            base = spread - jnp.mean(spread, axis=1, keepdims=True)
            hi, lo = split(base)
            cross = split((dot_nt(hi, earlier_low) + dot_nt(lo, earlier_low)) / (members - 1))
            spread = spread + jnp.dot(cross[0], earlier_weights, preferred_element_type=F32)
            spread = spread + jnp.dot(cross[1], earlier_weights, preferred_element_type=F32)
        mismatch = pert[b].astype(F32) - spread
        if history:
            spread = spread - jnp.mean(spread, axis=1, keepdims=True)
        spread_low = spread.astype(BF16)
        gain = (dot_nt(anom, spread_low) / (members - 1)).astype(BF16)
        weights = newton_weights(spread_low, mismatch, offsets[b], b)
        low = (state + jnp.dot(gain, weights, preferred_element_type=F32)).astype(BF16)
        history.append((spread_low, weights))
        if b + 1 < batches:
            state = low.astype(F32)
            anom = anomaly(state)
    out_ref[...] = low
    for copy in sends:
        copy.wait_send()


def on_device(ensemble, tiles, tile_live, observed, perturb, obs_var):
    region_count = lax.axis_size("region")
    group_count = lax.axis_size("group")
    batches, obs_count, members = perturb.shape
    chunk_rows = max(16, obs_count // region_count)
    chunk_cols = obs_count * members // (region_count * chunk_rows)
    vmem = pl.BlockSpec(memory_space=pltpu.VMEM)
    hbm = pl.BlockSpec(memory_space=pl.ANY)
    block = (chunk_rows, chunk_cols)
    dma = pltpu.SemaphoreType.DMA
    return pl.pallas_call(
        functools.partial(kernel, region_count, group_count),
        out_shape=jax.ShapeDtypeStruct(ensemble.shape, ensemble.dtype),
        in_specs=[hbm, hbm, pl.BlockSpec(memory_space=pltpu.SMEM), vmem, hbm, vmem],
        out_specs=vmem,
        scratch_shapes=[
            pltpu.VMEM(ensemble.shape, BF16),
            pltpu.VMEM(tiles.shape, BF16),
            pltpu.VMEM(perturb.shape, BF16),
            pltpu.VMEM(perturb.shape, BF16),
            pltpu.VMEM((batches, region_count, *block), BF16),
            pltpu.VMEM((batches, *block), BF16),
            pltpu.VMEM((batches, group_count, *block), BF16),
            pltpu.VMEM(perturb.shape, BF16),
            pltpu.VMEM((1, batches * obs_count), F32),
            pltpu.VMEM((region_count, 1, batches * obs_count), F32),
            pltpu.VMEM((1, batches * obs_count), F32),
            pltpu.VMEM((group_count, 1, batches * obs_count), F32),
            dma((1 + 2 * batches,)),
            dma((batches, region_count)),
            dma((batches, region_count)),
            dma((batches, group_count)),
            dma((batches, group_count)),
            dma((batches, region_count)),
            dma((batches, region_count)),
            dma((region_count,)),
            dma((region_count,)),
            dma((group_count,)),
            dma((group_count,)),
        ],
        compiler_params=pltpu.CompilerParams(collective_id=0, has_side_effects=True),
    )(ensemble, tiles, tile_live, observed, perturb, obs_var)


def solution(mesh):
    return jax.shard_map(
        on_device,
        mesh=mesh,
        in_specs=(
            P(("region", "group"), None),
            P(None, None, ("region", "group")),
            P(),
            P(),
            P(),
            P(),
        ),
        out_specs=P(("region", "group"), None),
        check_vma=False,
    )
```

```python
import functools

import jax
import jax.numpy as jnp
from jax import lax
from jax.experimental import pallas as pl
from jax.experimental.pallas import tpu as pltpu
from jax.sharding import PartitionSpec as P

NEWTON = 4
CORES = 2
PIECES = 2
F32 = jnp.float32
BF16 = jnp.bfloat16


def split(x):
    hi = x.astype(BF16)
    return hi, (x - hi.astype(F32)).astype(BF16)


def dot3(a, b):
    left = jnp.concatenate([a[0], a[0], a[1]], axis=1)
    right = jnp.concatenate([b[0], b[1], b[0]], axis=0)
    return jnp.dot(left, right, preferred_element_type=F32)


def dot_nt(a, b):
    return lax.dot_general(a, b, (((1,), (1,)), ((), ())), preferred_element_type=F32)


def kernel(
    region_count, group_count,
    ens_hbm, tiles_hbm, live_ref, obs_ref, pert_hbm, var_ref,
    out_ref,
    ens, tiles, pert, partial, rs_buf, z_send, z_buf, spread_buf,
    mean_part, mean_rs, mean_zsend, mean_z,
    pair_buf, half_buf,
    load_sem, rs_ssem, rs_rsem, z_ssem, z_rsem, ag_ssem, ag_rsem,
    mrs_ssem, mrs_rsem, mz_ssem, mz_rsem, pair_ssem, pair_rsem,
):
    batches, obs_count, members = pert.shape
    region = lax.axis_index("region")
    group = lax.axis_index("group")
    chunk_rows, chunk_cols = rs_buf.shape[2:]
    across = members // chunk_cols

    barrier = pltpu.get_barrier_semaphore()
    for k in range(1, region_count):
        pl.semaphore_signal(barrier, inc=1, device_id=(lax.rem(region + k, region_count), group), device_id_type=pl.DeviceIdType.MESH)
    for k in range(1, group_count):
        pl.semaphore_signal(barrier, inc=1, device_id=(region, lax.rem(group + k, group_count)), device_id_type=pl.DeviceIdType.MESH)

    loads = [pltpu.make_async_copy(ens_hbm, ens, load_sem.at[0])]
    loads += [pltpu.make_async_copy(tiles_hbm.at[b], tiles.at[b], load_sem.at[1 + b]) for b in range(batches)]
    loads += [pltpu.make_async_copy(pert_hbm.at[b], pert.at[b], load_sem.at[1 + batches + b]) for b in range(batches)]
    for load in loads[:1 + batches]:
        load.start()

    row_at = lax.broadcasted_iota(jnp.int32, (obs_count, obs_count), 0)
    col_at = lax.broadcasted_iota(jnp.int32, (obs_count, obs_count), 1)
    on_diag = row_at == col_at
    ident = jnp.where(on_diag, 1.0, 0.0).astype(F32)

    def as_row(column):
        return jnp.sum(jnp.where(on_diag, column, 0.0), axis=0, keepdims=True)

    def as_column(row):
        return jnp.sum(jnp.where(on_diag, row, 0.0), axis=1, keepdims=True)

    piece_cols = chunk_cols // PIECES

    def chunk(ref, index, piece=None):
        rows = pl.ds(pl.multiple_of(lax.div(index, across) * chunk_rows, chunk_rows), chunk_rows)
        start, width = (0, chunk_cols) if piece is None else (piece * piece_cols, piece_cols)
        if across > 1:
            start = pl.multiple_of(lax.rem(index, across) * chunk_cols + start, piece_cols)
        return ref.at[rows, pl.ds(start, width)]

    def part(ref, piece):
        return ref if piece is None else ref.at[:, pl.ds(piece * piece_cols, piece_cols)]

    def sem_row(b, piece):
        return b * PIECES + (piece or 0)

    def pieces_of(b):
        return range(PIECES) if b == 0 else (None,)

    def remote(src, dst, ssem, rsem, where):
        return pltpu.make_async_remote_copy(
            src_ref=src, dst_ref=dst, send_sem=ssem, recv_sem=rsem,
            device_id=where, device_id_type=pl.DeviceIdType.MESH,
        )

    region_peers = [lax.rem(region + k, region_count) for k in range(1, region_count)]
    group_peers = [lax.rem(group + k, group_count) for k in range(1, group_count)]
    sends = []

    def launch(copy):
        copy.start()
        sends.append(copy)

    def local_partial(b):
        loads[1 + b].wait()
        value = jnp.dot(tiles[b], ens[...], preferred_element_type=F32)
        value = value * live_ref[b, region].astype(F32)
        mean = jnp.mean(value, axis=1, keepdims=True)
        partial[b] = (value - mean).astype(BF16)
        return mean

    chips = region_count // CORES
    chip, core = lax.div(region, CORES), lax.rem(region, CORES)
    chip_order = [lax.rem(chip + 1 + k, chips) for k in range(chips)]
    chip_peers = chip_order[:-1]
    partner = chip * CORES + (CORES - 1 - core)

    def scatter(b, piece):
        row = sem_row(b, piece)
        for k, peer in enumerate(region_peers):
            launch(remote(chunk(partial.at[b], peer, piece), part(rs_buf.at[b, region], piece), rs_ssem.at[row, k], rs_rsem.at[row, region], (peer, group)))

    def scatter_pair(b):
        for k, there in enumerate(chip_order):
            launch(remote(chunk(partial.at[b], there * CORES + CORES - 1 - core), pair_buf.at[b, there], pair_ssem.at[b, k], pair_rsem.at[b, there], (partner, group)))

    def pair_sum(b, there):
        remote(pair_buf.at[b, there], pair_buf.at[b, there], pair_ssem.at[b, 0], pair_rsem.at[b, there], (partner, group)).wait_recv()
        return chunk(partial.at[b], there * CORES + core)[...].astype(F32) + pair_buf[b, there].astype(F32)

    def scatter_chips(b):
        row = sem_row(b, None)
        for k, there in enumerate(chip_peers):
            half_buf[b, there] = pair_sum(b, there).astype(BF16)
            launch(remote(half_buf.at[b, there], rs_buf.at[b, region], rs_ssem.at[row, k], rs_rsem.at[row, region], (there * CORES + core, group)))

    def sum_region(b, piece):
        row = sem_row(b, piece)
        if b == 0:
            total, peers = chunk(partial.at[b], region, piece)[...].astype(F32), region_peers
        else:
            total, peers = pair_sum(b, chip), [there * CORES + core for there in chip_peers]
        for peer in peers:
            block = part(rs_buf.at[b, peer], piece)
            remote(block, block, rs_ssem.at[row, 0], rs_rsem.at[row, peer], (peer, group)).wait_recv()
            total = total + block[...].astype(F32)
        mine = part(z_send.at[b], piece)
        mine[...] = total.astype(BF16)
        for k, peer in enumerate(group_peers):
            launch(remote(mine, part(z_buf.at[b, group], piece), z_ssem.at[row, k], z_rsem.at[row, group], (region, peer)))

    def sum_group(b, piece):
        row = sem_row(b, piece)
        total = part(z_send.at[b], piece)[...].astype(F32)
        for peer in group_peers:
            block = part(z_buf.at[b, peer], piece)
            remote(block, block, z_ssem.at[row, 0], z_rsem.at[row, peer], (region, peer)).wait_recv()
            total = total + block[...].astype(F32)
        mine = chunk(spread_buf.at[b], region, piece)
        mine[...] = total.astype(BF16)
        for k, peer in enumerate(region_peers):
            launch(remote(mine, mine, ag_ssem.at[row, k], ag_rsem.at[row, region], (peer, group)))

    def gathered(b):
        for piece in pieces_of(b):
            for peer in region_peers:
                block = chunk(spread_buf.at[b], peer, piece)
                row = sem_row(b, piece)
                remote(block, block, ag_ssem.at[row, 0], ag_rsem.at[row, peer], (peer, group)).wait_recv()
        return spread_buf[b]

    loads[0].wait()
    means = [local_partial(0)]
    pl.semaphore_wait(barrier, region_count - 1 + group_count - 1)
    for piece in pieces_of(0):
        scatter(0, piece)
    for load in loads[1 + batches:]:
        load.start()
    for b in range(1, batches):
        means.append(local_partial(b))
    for b in range(1, batches):
        scatter_pair(b)
    for b in range(batches):
        mean_part[:, b * obs_count:(b + 1) * obs_count] = as_row(means[b])
    for k, peer in enumerate(region_peers):
        launch(remote(mean_part, mean_rs.at[region], mrs_ssem.at[k], mrs_rsem.at[region], (peer, group)))
    for b in range(1, batches):
        scatter_chips(b)
    for piece in pieces_of(0):
        sum_region(0, piece)
    total = mean_part[...]
    for peer in region_peers:
        remote(mean_rs.at[peer], mean_rs.at[peer], mrs_ssem.at[0], mrs_rsem.at[peer], (peer, group)).wait_recv()
        total = total + mean_rs[peer]
    mean_zsend[...] = total
    for k, peer in enumerate(group_peers):
        launch(remote(mean_zsend, mean_z.at[group], mz_ssem.at[k], mz_rsem.at[group], (region, peer)))
    for b in range(1, batches):
        sum_region(b, None)
    for piece in pieces_of(0):
        sum_group(0, piece)
    mean_row = mean_zsend[...]
    for peer in group_peers:
        remote(mean_z.at[peer], mean_z.at[peer], mz_ssem.at[0], mz_rsem.at[peer], (region, peer)).wait_recv()
        mean_row = mean_row + mean_z[peer]
    for b in range(1, batches):
        sum_group(b, None)

    def anomaly(wide):
        return (wide - jnp.mean(wide, axis=1, keepdims=True)).astype(BF16)

    def newton_weights(spread_low, mismatch, shift, b):
        cov = dot_nt(spread_low, spread_low) / (members - 1) + jnp.where(on_diag, var_ref[b:b + 1, :], 0.0)
        bound = jnp.max(jnp.sum(jnp.abs(cov), axis=1, keepdims=True), axis=0, keepdims=True)
        residual = ident - cov / bound
        approx = ident + residual
        for step in range(1, NEWTON):
            parts = split(residual)
            residual = dot3(parts, parts)
            approx = approx + dot3(split(approx), split(residual))
        innov = mismatch + shift
        return (dot3(split(approx), split(innov)) / bound).astype(BF16)

    state = ens[...].astype(F32)
    anom = anomaly(state)
    offsets = [
        as_column(obs_ref[b:b + 1, :] - mean_row[:, b * obs_count:(b + 1) * obs_count]) for b in range(batches)
    ]
    history = []
    for b in range(batches):
        loads[1 + batches + b].wait()
        prior = gathered(b)
        spread = prior.astype(F32)
        for earlier_low, earlier_weights in history:
            base = spread - jnp.mean(spread, axis=1, keepdims=True)
            hi, lo = split(base)
            cross = split((dot_nt(hi, earlier_low) + dot_nt(lo, earlier_low)) / (members - 1))
            spread = spread + jnp.dot(cross[0], earlier_weights, preferred_element_type=F32)
            spread = spread + jnp.dot(cross[1], earlier_weights, preferred_element_type=F32)
        mismatch = pert[b].astype(F32) - spread
        if history:
            spread = spread - jnp.mean(spread, axis=1, keepdims=True)
        spread_low = spread.astype(BF16)
        gain = (dot_nt(anom, spread_low) / (members - 1)).astype(BF16)
        weights = newton_weights(spread_low, mismatch, offsets[b], b)
        low = (state + jnp.dot(gain, weights, preferred_element_type=F32)).astype(BF16)
        history.append((spread_low, weights))
        if b + 1 < batches:
            state = low.astype(F32)
            anom = anomaly(state)
    out_ref[...] = low
    for copy in sends:
        copy.wait_send()


def on_device(ensemble, tiles, tile_live, observed, perturb, obs_var):
    region_count = lax.axis_size("region")
    group_count = lax.axis_size("group")
    batches, obs_count, members = perturb.shape
    chunk_rows = max(16, obs_count // region_count)
    chunk_cols = obs_count * members // (region_count * chunk_rows)
    vmem = pl.BlockSpec(memory_space=pltpu.VMEM)
    hbm = pl.BlockSpec(memory_space=pl.ANY)
    block = (chunk_rows, chunk_cols)
    dma = pltpu.SemaphoreType.DMA
    return pl.pallas_call(
        functools.partial(kernel, region_count, group_count),
        out_shape=pltpu.VMEM(ensemble.shape, ensemble.dtype),
        in_specs=[hbm, hbm, pl.BlockSpec(memory_space=pltpu.SMEM), vmem, hbm, vmem],
        out_specs=vmem,
        scratch_shapes=[
            pltpu.VMEM(ensemble.shape, BF16),
            pltpu.VMEM(tiles.shape, BF16),
            pltpu.VMEM(perturb.shape, BF16),
            pltpu.VMEM(perturb.shape, BF16),
            pltpu.VMEM((batches, region_count, *block), BF16),
            pltpu.VMEM((batches, *block), BF16),
            pltpu.VMEM((batches, group_count, *block), BF16),
            pltpu.VMEM(perturb.shape, BF16),
            pltpu.VMEM((1, batches * obs_count), F32),
            pltpu.VMEM((region_count, 1, batches * obs_count), F32),
            pltpu.VMEM((1, batches * obs_count), F32),
            pltpu.VMEM((group_count, 1, batches * obs_count), F32),
            pltpu.VMEM((batches, region_count // CORES, *block), BF16),
            pltpu.VMEM((batches, region_count // CORES, *block), BF16),
            dma((1 + 2 * batches,)),
            dma((batches * PIECES, region_count)),
            dma((batches * PIECES, region_count)),
            dma((batches * PIECES, group_count)),
            dma((batches * PIECES, group_count)),
            dma((batches * PIECES, region_count)),
            dma((batches * PIECES, region_count)),
            dma((region_count,)),
            dma((region_count,)),
            dma((group_count,)),
            dma((group_count,)),
            dma((batches, region_count // CORES)),
            dma((batches, region_count // CORES)),
        ],
        compiler_params=pltpu.CompilerParams(collective_id=0, has_side_effects=True),
    )(ensemble, tiles, tile_live, observed, perturb, obs_var)


def solution(mesh):
    return jax.shard_map(
        on_device,
        mesh=mesh,
        in_specs=(
            P(("region", "group"), None),
            P(None, None, ("region", "group")),
            P(),
            P(),
            P(),
            P(),
        ),
        out_specs=P(("region", "group"), None),
        check_vma=False,
    )
```
